128 devices in a mesh: piece: 32 (over y, x, core), col: 4 (over z).
Axes of the slice: x: 4, y: 4, z: 4, core: 2. Of those that a mesh axis runs over, the one named last changes fastest.
Arguments:
- positions: float32 [3, 4096, 128], P(None, 'piece'), as said below
- phase: int32 [4096, 128], P('piece'), may hold values from 0 to 2
- neighbours: int32 [4096, 28], P('piece', 'col'), may hold values from -1 to 4095, as said below
- counts: int32 [32], replicated, may hold values from 64 to 128, as said below
- phase_density: float32 [3], replicated, may hold values from 0.1 to 1
- right_side: float32 [4096, 128], P(('piece', 'col')), may hold values from -6 to 6
Outputs:
- solution_field: float32 [4096, 128], P(('piece', 'col'))
- residual: float32 [4096, 128], P(('piece', 'col'))
The draws below stay inside these ranges and needn't reach their ends.
Inputs may be any that keep to these rules, and one draw needn't show every extreme that they name: `neighbours`: the slots of each piece at or past its count hold no block. Live blocks, taken in slot order piece after piece, form layers of 16 blocks in Morton order of a 4 x 4 grid. Block q lists n exactly when n lists q; every listed block lies on q's own piece or the piece just before or after it, and its place in that order of live blocks differs from q's by less than 32; empty slots and the last column list only -1. `counts`: some piece holds exactly 128 live blocks. `positions`: the particles of one live block lie in one unit cell; particles of two live blocks that do not list each other are 1 or more apart.
All inputs are finite; a program needn't handle non-finite values.
Results may differ from the reference program's by a relative error of at most 0.0003.
Values sent between devices are 32-bit elements; how exact they have to be, the bound alone decides.
A program may use at most 64 MiB of HBM per device.

```python
import math
import jax
import jax.numpy as jnp
from jax import lax

BLK = 128
SIDE = 4
LAYER = 16
CAP = 128
NEIGHBOUR_SLOTS = 28
ITERS = 2
NBLK = 4096
N_PIECE = 32


def layout_counts(key):
    first_key = jax.random.fold_in(key, 101)
    second_key = jax.random.fold_in(key, 102)
    extra = jax.random.randint(first_key, (N_PIECE,), 0, CAP // 2 + 1)
    filled = CAP // 2 + extra
    chosen = jax.random.randint(second_key, (), 0, N_PIECE)
    filled = jnp.where(jnp.arange(N_PIECE, dtype=jnp.int32) == chosen, CAP, filled).astype(jnp.int32)
    starts = (jnp.cumsum(filled) - filled).astype(jnp.int32)
    return (filled, starts)


def morton_cell(code):
    levels = SIDE.bit_length() - 1
    across = jnp.zeros_like(code)
    along = jnp.zeros_like(code)
    for level in range(levels):
        across = across + code // 4 ** level % 2 * 2 ** level
        along = along + code // (2 * 4 ** level) % 2 * 2 ** level
    return (across, along)


def morton_code(across, along):
    levels = SIDE.bit_length() - 1
    code = jnp.zeros_like(across)
    for level in range(levels):
        code = code + across // 2 ** level % 2 * 4 ** level
        code = code + along // 2 ** level % 2 * (2 * 4 ** level)
    return code


def slot_cells(key):
    filled, starts = layout_counts(key)
    slots = jnp.arange(NBLK, dtype=jnp.int32)
    owner = slots // CAP
    within = slots % CAP
    live = within < filled[owner]
    dense = starts[owner] + within
    height = dense // LAYER
    across, along = morton_cell(dense % LAYER)
    return (filled, starts, live, height, across, along)


def draw_counts(key, part):
    return layout_counts(key)[0]


def draw_neighbours(key, part):
    filled, starts, live, height, across, along = slot_cells(key)
    total = jnp.sum(filled)
    columns = []
    for step_z in (-1, 0, 1):
        for step_y in (-1, 0, 1):
            for step_x in (-1, 0, 1):
                next_x = across + step_x
                next_y = along + step_y
                next_z = height + step_z
                inside = (next_x >= 0) & (next_x < SIDE) & (next_y >= 0) & (next_y < SIDE) & (next_z >= 0)
                target = next_z * LAYER + morton_code(jnp.clip(next_x, 0, SIDE - 1), jnp.clip(next_y, 0, SIDE - 1))
                inside = inside & (target < total) & live
                holder = jnp.sum((starts[None, :] <= target[:, None]).astype(jnp.int32), axis=1) - 1
                holder = jnp.clip(holder, 0, N_PIECE - 1)
                worldwide_slot = holder * CAP + target - starts[holder]
                columns.append(jnp.where(inside, worldwide_slot, -1))
    columns.append(jnp.full((NBLK,), -1, jnp.int32))
    return jnp.stack(columns, axis=1).astype(jnp.int32)


def draw_positions(key, part):
    filled, starts, live, height, across, along = slot_cells(key)
    offsets = jax.random.uniform(jax.random.fold_in(key, 103), (3, NBLK, BLK), jnp.float32)
    corner = jnp.stack([across, along, height], 0).astype(jnp.float32)
    return (corner[:, :, None] + offsets).astype(jnp.float32)


def touch_ends(array, own_key, least, top_value):
    shape = array.shape
    index_at = [jax.random.randint(jax.random.fold_in(own_key, axis), (), 0, shape[axis]) for axis in range(len(shape))]
    array = array.at[tuple(index_at)].set(least)
    longest = shape.index(max(shape))
    index_at[longest] = (index_at[longest] + 1) % shape[longest]
    return array.at[tuple(index_at)].set(top_value)


def block_scale(stream_key, shape, shards, least, largest):
    def one(position, blocks):
        draws = jax.random.uniform(jax.random.fold_in(jax.random.fold_in(stream_key, 6), position), (blocks,), jnp.float32, least / len(shards), largest / len(shards))
        return jnp.repeat(jnp.exp(draws), shape[position] // blocks).reshape((-1,) + (1,) * (len(shape) - position - 1))

    factor_of = one(*shards[0])
    for cut in shards[1:]:
        factor_of = factor_of * one(*cut)
    return factor_of


def scatter_about(stream_key, extent, spread, most, pieces=(), kind=jnp.bfloat16):
    gain = block_scale(stream_key, extent, pieces, -0.22, 0.18) if pieces else 1.0
    entries = jax.random.normal(stream_key, extent, jnp.float32) * spread * gain
    return jnp.minimum(jnp.maximum(entries, -most), most).astype(kind)


def setup_inputs(seed: int = 0) -> dict:
    key_list = jax.random.split(jax.random.key(seed), 7)
    positions = draw_positions(jax.random.fold_in(key_list[6], 71), 0)
    phase = touch_ends(jax.random.randint(key_list[1], (NBLK, BLK), 0, 3), jax.random.fold_in(key_list[1], 1), 0, 2).astype(jnp.int32)
    neighbours = draw_neighbours(jax.random.fold_in(key_list[6], 71), 0)
    counts = draw_counts(jax.random.fold_in(key_list[6], 71), 0)
    phase_density = jnp.clip(jnp.exp(jax.random.uniform(key_list[4], (3,), jnp.float32, math.log(0.1), math.log(1.0))), 0.1, 1.0)
    right_side = scatter_about(key_list[5], (NBLK, BLK), 1.0, 6.0, ((0, 128),), jnp.float32)
    return dict(positions=positions, phase=phase, neighbours=neighbours, counts=counts, phase_density=phase_density, right_side=right_side)


def fetch_phase_density(phase, phase_density):
    labels = jnp.arange(3, dtype=jnp.int32)
    return jnp.sum(jnp.where(phase[..., None] == labels, phase_density, 0.0), axis=-1).astype(jnp.float32)


def pair_term(own_pos, own_rho, own_ids, slot_ids, hood_state, hood_field, base):
    valid = slot_ids >= 0
    where_at = jnp.clip(slot_ids - base, 0, hood_field.shape[0] - 1).astype(jnp.int32)
    other = hood_state[:, where_at]
    remote = hood_field[where_at]
    squared = jnp.zeros((own_rho.shape[0], own_rho.shape[1], own_rho.shape[1]), jnp.float32)
    for component in range(3):
        slot_displacement = own_pos[component][:, :, None] - other[component][:, None, :]
        squared = squared + slot_displacement * slot_displacement
    kernel = jnp.square(jnp.maximum(1.0 - squared, 0.0)) / (squared + 0.01)
    weight = 2.0 / (own_rho[:, :, None] + other[3][:, None, :])
    particles = jnp.arange(own_rho.shape[1], dtype=jnp.int32)
    same = (slot_ids == own_ids)[:, None, None] & (particles[:, None] == particles[None, :])[None]
    keep = valid[:, None, None] & jnp.logical_not(same)
    tile = jnp.where(keep, kernel * weight / own_rho.shape[1], 0.0)
    return jnp.einsum("gij,gj->gi", tile, remote, precision=lax.Precision.HIGHEST)


def reference(positions, phase, neighbours, counts, phase_density, right_side):
    density = fetch_phase_density(phase, phase_density)
    state = jnp.concatenate([positions, density[None]], 0)
    slots = jnp.arange(NBLK, dtype=jnp.int32)
    live = (slots % CAP) < counts[slots // CAP]
    source = jnp.where(live[:, None], right_side, 0.0)
    group = 16

    def apply_pairs(field):
        def group_sum(start):
            own_pos = lax.dynamic_slice_in_dim(positions, start, group, 1)
            own_rho = lax.dynamic_slice_in_dim(density, start, group, 0)
            own_ids = start + jnp.arange(group, dtype=jnp.int32)
            lists = lax.dynamic_slice_in_dim(neighbours, start, group, 0)
            running = jnp.zeros((group, BLK), jnp.float32)
            for neighbour_slot in range(NEIGHBOUR_SLOTS):
                running = running + pair_term(own_pos, own_rho, own_ids, lists[:, neighbour_slot], state, field, 0)
            return running
        starts = jnp.arange(NBLK // group, dtype=jnp.int32) * group
        return lax.map(group_sum, starts).reshape(NBLK, BLK)

    diagonal = 1.0 / density + apply_pairs(jnp.ones((NBLK, BLK), jnp.float32))
    solution_field = jnp.zeros((NBLK, BLK), jnp.float32)
    residual = source
    precond = residual / diagonal
    direction = precond
    weighted = jnp.sum(residual * precond)
    for step in range(ITERS):
        image = diagonal * direction - apply_pairs(direction)
        advance = weighted / jnp.sum(direction * image)
        solution_field = solution_field + advance * direction
        residual = residual - advance * image
        precond = residual / diagonal
        weighted_next = jnp.sum(residual * precond)
        direction = precond + (weighted_next / weighted) * direction
        weighted = weighted_next
    return solution_field, residual
```

```python
import functools

import jax
import jax.numpy as jnp
import numpy as np
from jax import lax
from jax.experimental import pallas as pl
from jax.experimental.pallas import tpu as pltpu
from jax.sharding import PartitionSpec as P

MESH = pl.DeviceIdType.MESH
BLK = 128
CAP = 128
LAYER = 16
SHARE = 32
FAR = 1.0e4
FAR_NULL = 2.0e4
STATE_NULL = 192
FIELD_NULL = 256


def layer_cells():
    place = []
    for code in range(LAYER):
        across = code % 2 + 2 * (code // 4 % 2)
        along = code // 2 % 2 + 2 * (code // 8 % 2)
        place.append((across, along))
    near = []
    for code in range(LAYER):
        others = [
            other
            for other in range(LAYER)
            if other != code
            and abs(place[other][0] - place[code][0]) <= 1
            and abs(place[other][1] - place[code][1]) <= 1
        ]
        near.append([code] + others)
    return near


NEAR = layer_cells()
CELLS = sorted(range(LAYER), key=lambda code: (len(NEAR[code]), code))


def tile_plan():
    rows, groups = [], []
    own_cell, own_half = [], []
    for degree in (4, 6, 9):
        cells = [code for code in CELLS if len(NEAR[code]) == degree]
        groups.append((degree, len(own_cell), 2 * len(cells), len(rows)))
        for code in cells:
            for half in range(2):
                own_cell.append(code)
                own_half.append(half)
                for kind in range(3):
                    for other in NEAR[code]:
                        rows.append((code, half, kind, other))
    return np.array(rows, np.int32), groups, np.array(own_cell, np.int32), np.array(own_half, np.int32)


ROWS, GROUPS, OWN_CELL, OWN_HALF = tile_plan()
TILES = ROWS.shape[0]
UNITS = 2 * LAYER
RANK_OF = np.zeros((LAYER,), np.int32)
for _rank, _code in enumerate(CELLS):
    RANK_OF[_code] = _rank


def tables(counts, piece, column):
    lanes = jnp.arange(counts.shape[0], dtype=jnp.int32)
    start = jnp.sum(jnp.where(lanes < piece, counts, 0))
    total = jnp.sum(counts)
    filled = jnp.sum(jnp.where(lanes == piece, counts, 0))
    before = jnp.sum(jnp.where(lanes == piece - 1, counts, 0))
    first = start + SHARE * column

    def local(cell, half):
        return (cell - first) % LAYER + LAYER * half

    cell, half, kind, other = (jnp.asarray(ROWS[:, i]) for i in range(4))
    own = local(cell, half)
    mate = local(other, half)
    level = (first + own) // LAYER
    lift = (first + mate) // LAYER - level
    step = jnp.where(
        kind == 0, lift, jnp.where(kind == 1, jnp.where(lift == -1, 0, -1), jnp.where(lift == 1, 0, 1))
    )
    order = LAYER * (level + step) + other
    slot = order - start
    good = (order >= 0) & (order < total) & (SHARE * column + own < filled)
    state_at = jnp.where(slot < filled, SHARE + slot, SHARE + CAP + slot - filled)
    state_at = jnp.where(good, state_at, STATE_NULL)
    field_at = jnp.where(
        slot < 0,
        before + slot - SHARE,
        jnp.where(slot < filled, 3 * SHARE + slot, 3 * SHARE + CAP + slot - filled),
    )
    field_at = jnp.where(good, field_at, FIELD_NULL)
    units = local(jnp.asarray(OWN_CELL), jnp.asarray(OWN_HALF))
    spots = jnp.arange(UNITS, dtype=jnp.int32)
    cell_of = (first + spots) % LAYER
    rank_of = jnp.sum(
        jnp.where(cell_of[:, None] == jnp.arange(LAYER)[None], jnp.asarray(RANK_OF)[None], 0), axis=1
    )
    unit_of = 2 * rank_of + spots // LAYER
    return jnp.concatenate([state_at, field_at, units, unit_of, filled[None]]).astype(jnp.int32)


FIELD_TAB = TILES
UNIT_TAB = 2 * TILES
SPOT_TAB = 2 * TILES + UNITS
FILLED_TAB = 2 * TILES + 2 * UNITS


def kernel(
    pieces, columns,
    tab, dens, pos_ref, phase_ref, near_ref, rhs_ref,
    x_ref, r_ref,
    state, spread, tiles, listed, listed_in, head, tail, density,
    own_z, own_t, hood_z, hood_t, rowbuf, diag, y0, y1, moments, stage_a, stage_b,
    state_send, state_recv, list_send, list_recv, z_send, z_recv, t_send, t_recv, a_send, a_recv, b_send, b_recv,
):
    piece = lax.axis_index("piece")
    column = lax.axis_index("col")
    after = lax.rem(piece + 1, pieces)
    ahead = lax.rem(piece + pieces - 1, pieces)
    core = lax.rem(piece, 2)
    chip = piece // 2
    rank_a = column * 2 + core

    def member_a(rank):
        return (chip * 2 + lax.rem(rank, 2), rank // 2)

    def member_b(rank):
        return (rank * 2 + core, column)

    barrier = pltpu.get_barrier_semaphore()

    def greet(target):
        pl.semaphore_signal(barrier, inc=1, device_id=target, device_id_type=MESH)

    greet((after, column))
    greet((ahead, column))
    for step in range(1, columns):
        greet((piece, lax.rem(column + step, columns)))
    for step in range(1, 8):
        greet(member_a(lax.rem(rank_a + step, 8)))
    for step in range(1, 16):
        greet(member_b(lax.rem(chip + step, 16)))

    @pl.when(column == 0)
    def _():
        for other in range(1, columns):
            greet((ahead, other))

    @pl.when(column > 0)
    def _():
        greet((after, 0))

    filled = tab[FILLED_TAB]
    slots = lax.broadcasted_iota(jnp.int32, (CAP, BLK), 0)
    live = slots < filled
    for axis in range(3):
        state[axis, SHARE : SHARE + CAP, :] = jnp.where(live, pos_ref[axis], FAR)
        state[axis, STATE_NULL : STATE_NULL + 8, :] = jnp.full((8, BLK), FAR_NULL, jnp.float32)
    phase = phase_ref[...]
    scaled = jnp.where(phase == 0, dens[0], jnp.where(phase == 1, dens[1], dens[2])) * 64.0
    state[3, SHARE : SHARE + CAP, :] = jnp.where(live, scaled, 64.0)
    state[3, STATE_NULL : STATE_NULL + 8, :] = jnp.full((8, BLK), 64.0, jnp.float32)

    near = near_ref[...]
    me_at = lax.broadcasted_iota(jnp.int32, near.shape, 0) + piece * CAP
    hits = jnp.sum(jnp.where(near == me_at, 1.0, 0.0), axis=1, keepdims=True)
    listed[...] = jnp.broadcast_to(hits, (CAP, BLK))

    for axis in range(4):
        head[axis] = state[axis, SHARE : 2 * SHARE, :]

    density[...] = scaled

    def tail_row(row, carry):
        at = jnp.clip(filled - SHARE, 0, CAP - SHARE) + row
        for axis in range(3):
            tail[axis, pl.ds(row, 1), :] = pos_ref[axis, pl.ds(at, 1), :]
        tail[3, pl.ds(row, 1), :] = density[pl.ds(at, 1), :]
        return carry

    lax.fori_loop(0, SHARE, tail_row, 0, unroll=4)

    hood_z[FIELD_NULL : FIELD_NULL + 8, :] = jnp.zeros((8, BLK), jnp.float32)
    hood_t[FIELD_NULL : FIELD_NULL + 8, :] = jnp.zeros((8, BLK), jnp.float32)

    @pl.when(column == 0)
    def _():
        pl.semaphore_wait(barrier, 2 + 3 + 7 + 15 + 3)

    @pl.when(column > 0)
    def _():
        pl.semaphore_wait(barrier, 2 + 3 + 7 + 15 + 1)

    def remote(source, target, send, recv, device):
        return pltpu.make_async_remote_copy(
            src_ref=source, dst_ref=target, send_sem=send, recv_sem=recv, device_id=device, device_id_type=MESH
        )

    to_after = remote(tail, state.at[:, 0:SHARE, :], state_send.at[0], state_recv.at[0], (after, column))
    to_ahead = remote(head, state.at[:, SHARE + CAP : 2 * SHARE + CAP, :], state_send.at[1], state_recv.at[1], (ahead, column))
    to_after.start()
    to_ahead.start()
    list_copies = []
    for step in range(1, columns):
        other = lax.rem(column + step, columns)
        copy = remote(
            listed.at[pl.ds(pl.multiple_of(other * SHARE, SHARE), SHARE), :],
            listed_in.at[step - 1],
            list_send.at[step - 1],
            list_recv.at[step - 1],
            (piece, other),
        )
        copy.start()
        list_copies.append(copy)
    to_after.wait()
    to_ahead.wait()
    for copy in list_copies:
        copy.wait()
    mine = listed[pl.ds(pl.multiple_of(column * SHARE, SHARE), SHARE), :]
    for step in range(columns - 1):
        mine = mine + listed_in[step]
    listed_in[0] = mine

    lane = lax.broadcasted_iota(jnp.int32, (8, BLK), 1)
    sublane = lax.broadcasted_iota(jnp.int32, (8, BLK), 0)

    def to_row(block):
        return jnp.sum(block.T, axis=0, keepdims=True)

    def weights(at, group):
        rows = slice(8 * group, 8 * group + 8)
        dx = spread[0, rows, :] - at[0]
        dy = spread[1, rows, :] - at[1]
        dz = spread[2, rows, :] - at[2]
        squared = dx * dx + dy * dy + dz * dz
        near_by = jnp.maximum(1.0 - squared, 0.0)
        below = (squared + 0.01) * (spread[3, rows, :] + at[3])
        inverse = pl.reciprocal(below, approx=True)
        inverse = inverse * (2.0 - below * inverse)
        return near_by * near_by * inverse

    def source_rows(where_at):
        return [jnp.broadcast_to(state[axis, pl.ds(where_at, 1), :], (8, BLK)) for axis in range(4)]

    for degree, unit_first, units, tile_first in GROUPS:
        per_unit = 3 * degree

        def unit_body(index, carry, per_unit=per_unit, unit_first=unit_first, tile_first=tile_first):
            unit = unit_first + index
            spot = tab[UNIT_TAB + unit]
            row = SHARE + SHARE * column + spot
            for axis in range(4):
                one = jnp.broadcast_to(state[axis, pl.ds(row, 1), :], (BLK, BLK))
                spread[axis] = one.T
            base = tile_first + index * per_unit
            at = source_rows(tab[base])
            often = jnp.broadcast_to(listed_in[0, pl.ds(spot, 1), :], (8, BLK))
            sums = []
            for group in range(16):
                weight = weights(at, group) * often
                weight = jnp.where(sublane + 8 * group == lane, 0.0, weight)
                tiles[base, 8 * group : 8 * group + 8, :] = weight
                sums.append(weight)

            def tile_body(k, sums):
                at = source_rows(tab[base + k])
                new = []
                for group in range(16):
                    weight = weights(at, group)
                    tiles[base + k, 8 * group : 8 * group + 8, :] = weight
                    new.append(sums[group] + weight)
                return tuple(new)

            sums = lax.fori_loop(1, per_unit, tile_body, tuple(sums))
            rowbuf[pl.ds(unit, 1), :] = to_row(jnp.concatenate(sums, axis=0))
            return carry

        lax.fori_loop(0, units, unit_body, 0)

    def settle(target):
        for spot in range(SHARE):
            target[spot : spot + 1, :] = rowbuf[pl.ds(tab[SPOT_TAB + spot], 1), :]

    settle(diag)
    own_at = pl.multiple_of(SHARE * column, SHARE)
    rho = state[3, pl.ds(pl.multiple_of(SHARE + own_at, SHARE), SHARE), :]
    alive = lax.broadcasted_iota(jnp.int32, (SHARE, BLK), 0) + own_at < filled
    diagonal = 64.0 / rho + diag[...]
    diag[...] = diagonal
    source = jnp.where(alive, rhs_ref[...], 0.0)
    z = source / diagonal

    def exchange(own, hood, send, recv):
        source_ref = own

        def chunk(at):
            return hood.at[pl.ds(pl.multiple_of(at, SHARE), SHARE), :]

        here = 3 * SHARE + SHARE * column
        cases = []
        cases.append((column < columns - 1, here, (piece, column + 1), 0, 0))
        cases.append((column > 0, here, (piece, column - 1), 1, 1))
        for other in range(1, columns):
            cases.append((column == 0, 3 * SHARE + CAP, (ahead, other), 1 + other, 2))
        for other in range(1, columns):
            cases.append((column == other, SHARE * (other - 1), (after, 0), 2, 2 + other))
        return source_ref, chunk, here, cases

    def start_exchange(own, hood, send, recv):
        source_ref, chunk, here, cases = exchange(own, hood, send, recv)
        for when, at, device, send_at, recv_at in cases:
            @pl.when(when)
            def _(at=at, device=device, send_at=send_at, recv_at=recv_at):
                remote(source_ref, chunk(at), send.at[send_at], recv.at[recv_at], device).start()

    def finish_exchange(own, hood, send, recv):
        source_ref, chunk, here, cases = exchange(own, hood, send, recv)
        arrive = [
            (column > 0, here - SHARE, 0),
            (column < columns - 1, here + SHARE, 1),
            (column > 0, 3 * SHARE + CAP, 2),
        ]
        for other in range(1, columns):
            arrive.append((column == 0, SHARE * (other - 1), 2 + other))
        for when, at, recv_at in arrive:
            @pl.when(when)
            def _(at=at, recv_at=recv_at):
                remote(source_ref, chunk(at), send.at[0], recv.at[recv_at], (after, column)).wait_recv()

        for when, at, device, send_at, recv_at in cases:
            @pl.when(when)
            def _(at=at, device=device, send_at=send_at, recv_at=recv_at):
                remote(source_ref, chunk(at), send.at[send_at], recv.at[recv_at], device).wait_send()

    def product(value, own, hood, send, recv):
        own[...] = value
        start_exchange(own, hood, send, recv)
        hood[pl.ds(pl.multiple_of(3 * SHARE + own_at, SHARE), SHARE), :] = value

        def gather(ref, base, count):
            return [
                jnp.broadcast_to(ref[pl.ds(tab[FIELD_TAB + base + k], 1), :], (8, BLK)) for k in range(count)
            ]

        finish_exchange(own, hood, send, recv)

        for degree, unit_first, units, tile_first in GROUPS:
            def unit_body(index, carry, degree=degree, unit_first=unit_first, tile_first=tile_first):
                unit = unit_first + index
                base = tile_first + index * (3 * degree)
                fields = gather(hood, base, 3 * degree)
                sums = []
                for group in range(16):
                    rows = slice(8 * group, 8 * group + 8)
                    total = tiles[base, rows, :] * fields[0]
                    for k in range(1, 3 * degree):
                        total = total + tiles[base + k, rows, :] * fields[k]
                    sums.append(total)
                rowbuf[pl.ds(unit, 1), :] = to_row(jnp.concatenate(sums, axis=0))
                return carry

            lax.fori_loop(0, units, unit_body, 0)

    product(z, own_z, hood_z, z_send, z_recv)
    settle(y0)
    t = y0[...] / diag[...]
    product(t, own_t, hood_t, t_send, t_recv)
    settle(y1)

    z = own_z[...]
    t = own_t[...]
    source = jnp.where(alive, rhs_ref[...], 0.0)

    def partial(first, second):
        return jnp.sum(first * second, axis=0, keepdims=True)

    moments[0:1, :] = partial(source, z)
    moments[1:2, :] = partial(z, y0[...])
    moments[2:3, :] = partial(y0[...], t)
    moments[3:4, :] = partial(t, y1[...])
    moments[4:8, :] = jnp.zeros((4, BLK), jnp.float32)

    def share_sums(from_ref, stage, rank, size, member, send, recv):
        copies = []
        for step in range(1, size):
            copy = remote(
                from_ref, stage.at[rank], send.at[step - 1], recv.at[step - 1], member(lax.rem(rank + step, size))
            )
            copy.start()
            copies.append(copy)
        stage[rank] = from_ref[...]
        for copy in copies:
            copy.wait()
        total = stage[0]
        for k in range(1, size):
            total = total + stage[k]
        return total

    moments[8:16, :] = share_sums(moments.at[0:8, :], stage_a, rank_a, 8, member_a, a_send, a_recv)
    total = share_sums(moments.at[8:16, :], stage_b, chip, 16, member_b, b_send, b_recv)
    sums = jnp.sum(total, axis=1, keepdims=True)
    e0, e1, e2, e3 = (sums[k : k + 1, :] for k in range(4))
    f1 = e1 / e0
    f2 = e2 / e0
    f3 = e3 / e0
    lead = 1.0 / (1.0 - f1)
    spread_of = f2 - f1 * f1
    ratio = lead * lead * spread_of
    bent = f3 - 2.0 * f1 * f2 + f1 * f1 * f1
    second = spread_of / (spread_of - bent - lead * spread_of * spread_of)
    mix = ratio - lead * f1
    first_image = y0[...]
    direction = lead * t + mix * z
    x_ref[...] = lead * z + second * direction
    image = (lead - mix) * first_image + mix * source - lead * y1[...]
    r_ref[...] = lead * (first_image - f1 * source) - second * image


def body(positions, phase, neighbours, counts, phase_density, right_side):
    pieces = lax.axis_size("piece")
    columns = lax.axis_size("col")
    table = tables(counts, lax.axis_index("piece"), lax.axis_index("col"))
    vmem = pl.BlockSpec(memory_space=pltpu.VMEM)
    smem = pl.BlockSpec(memory_space=pltpu.SMEM)
    f32 = jnp.float32
    dma = pltpu.SemaphoreType.DMA
    shape = jax.ShapeDtypeStruct((SHARE, BLK), f32)
    return pl.pallas_call(
        functools.partial(kernel, pieces, columns),
        out_shape=(shape, shape),
        in_specs=[smem, smem, vmem, vmem, vmem, vmem],
        out_specs=(vmem, vmem),
        scratch_shapes=[
            pltpu.VMEM((4, STATE_NULL + 8, BLK), f32),
            pltpu.VMEM((4, BLK, BLK), f32),
            pltpu.VMEM((TILES, BLK, BLK), f32),
            pltpu.VMEM((CAP, BLK), f32),
            pltpu.VMEM((3, SHARE, BLK), f32),
            pltpu.VMEM((4, SHARE, BLK), f32),
            pltpu.VMEM((4, SHARE, BLK), f32),
            pltpu.VMEM((CAP, BLK), f32),
            pltpu.VMEM((SHARE, BLK), f32),
            pltpu.VMEM((SHARE, BLK), f32),
            pltpu.VMEM((FIELD_NULL + 8, BLK), f32),
            pltpu.VMEM((FIELD_NULL + 8, BLK), f32),
            pltpu.VMEM((UNITS, BLK), f32),
            pltpu.VMEM((SHARE, BLK), f32),
            pltpu.VMEM((SHARE, BLK), f32),
            pltpu.VMEM((SHARE, BLK), f32),
            pltpu.VMEM((16, BLK), f32),
            pltpu.VMEM((8, 8, BLK), f32),
            pltpu.VMEM((16, 8, BLK), f32),
            dma((2,)), dma((2,)), dma((3,)), dma((3,)),
            dma((5,)), dma((6,)), dma((5,)), dma((6,)),
            dma((7,)), dma((7,)), dma((15,)), dma((15,)),
        ],
        compiler_params=pltpu.CompilerParams(
            collective_id=0, has_side_effects=True, vmem_limit_bytes=60 * 1024 * 1024
        ),
        name="pressure",
    )(table, phase_density, positions, phase, neighbours, right_side)


def solution(mesh):
    placed = (
        P(None, "piece", None),
        P("piece", None),
        P("piece", "col"),
        P(),
        P(),
        P(("piece", "col"), None),
    )
    return jax.shard_map(
        body,
        mesh=mesh,
        in_specs=placed,
        out_specs=(P(("piece", "col"), None), P(("piece", "col"), None)),
        check_vma=False,
    )
```

```python
import functools

import jax
import jax.numpy as jnp
from jax import lax
from jax.experimental import pallas as pl
from jax.experimental.pallas import tpu as pltpu
from jax.sharding import PartitionSpec as P

MESH = pl.DeviceIdType.MESH
BLK = 128
CAP = 128
LAYER = 16
SHARE = 32
HOOD = 3 * SHARE
FEATURES = 48
FAR = 64.0
STATE_NULL = 192
FIELD_NULL = 256
CELL_STEP = 10


def layer_cells():
    place = []
    for code in range(LAYER):
        across = code % 2 + 2 * (code // 4 % 2)
        along = code // 2 % 2 + 2 * (code // 8 % 2)
        place.append((across, along))
    near = []
    for code in range(LAYER):
        others = [
            other
            for other in range(LAYER)
            if other != code
            and abs(place[other][0] - place[code][0]) <= 1
            and abs(place[other][1] - place[code][1]) <= 1
        ]
        near.append([code] + others)
    return near


NEAR = layer_cells()
CELLS = sorted(range(LAYER), key=lambda code: (len(NEAR[code]), code))


def unit_plan():
    groups, first_unit, first_tile = [], 0, 0
    for degree in (4, 6, 9):
        units = 2 * len([code for code in CELLS if len(NEAR[code]) == degree])
        groups.append((degree, first_unit, units, first_tile))
        first_unit += units
        first_tile += 3 * degree * units
    return groups, first_unit, first_tile


GROUPS, UNITS, TILES = unit_plan()
PATTERN = [0] * (LAYER * CELL_STEP)
RANK_OF = [0] * LAYER
for _rank, _code in enumerate(CELLS):
    RANK_OF[_code] = _rank
    PATTERN[_rank * CELL_STEP : _rank * CELL_STEP + len(NEAR[_code])] = NEAR[_code]


def kernel(
    pieces, columns,
    counts, dens, pos_ref, phase_ref, near_ref, rhs_ref,
    x_ref, r_ref,
    pattern, rank_of, state_at, field_at,
    state, hood_state, right_rows, rho_rows, left_rows, right, left, tiles, listed, listed_in, head, tail, density,
    own_z, own_t, hood_z, hood_t, near_field, rowbuf, diag, y0, y1, moments, stage_a, stage_b,
    state_send, state_recv, list_send, list_recv, z_send, z_recv, t_send, t_recv, a_send, a_recv, b_send, b_recv,
):
    piece = lax.axis_index("piece")
    column = lax.axis_index("col")
    after = lax.rem(piece + 1, pieces)
    ahead = lax.rem(piece + pieces - 1, pieces)
    core = lax.rem(piece, 2)
    chip = piece // 2
    rank_a = column * 2 + core

    def member_a(rank):
        return (chip * 2 + lax.rem(rank, 2), rank // 2)

    def member_b(rank):
        return (rank * 2 + core, column)

    barrier = pltpu.get_barrier_semaphore()

    def greet(target):
        pl.semaphore_signal(barrier, inc=1, device_id=target, device_id_type=MESH)

    greet((after, column))
    greet((ahead, column))
    for step in range(1, columns):
        greet((piece, lax.rem(column + step, columns)))
    for step in range(1, 8):
        greet(member_a(lax.rem(rank_a + step, 8)))
    for step in range(1, 16):
        greet(member_b(lax.rem(chip + step, 16)))

    @pl.when(column == 0)
    def _():
        for other in range(1, columns):
            greet((ahead, other))

    @pl.when(column > 0)
    def _():
        greet((after, 0))

    start, total, filled, before = 0, 0, 0, 0
    for other in range(pieces):
        count = counts[other]
        start = start + jnp.where(other < piece, count, 0)
        total = total + count
        filled = filled + jnp.where(other == piece, count, 0)
        before = before + jnp.where(other == piece - 1, count, 0)
    first = start + SHARE * column
    for place, code in enumerate(PATTERN):
        pattern[place] = code
    for code in range(LAYER):
        rank_of[code] = RANK_OF[code]

    phase = phase_ref[...]
    scaled = jnp.where(phase == 0, dens[0], jnp.where(phase == 1, dens[1], dens[2])) * 64.0
    density[...] = scaled
    for axis in range(3):
        state[axis, SHARE : SHARE + CAP, :] = pos_ref[axis]
    state[3, SHARE : SHARE + CAP, :] = scaled

    near = near_ref[...]
    me_at = lax.broadcasted_iota(jnp.int32, near.shape, 0) + piece * CAP
    hits = jnp.sum(jnp.where(near == me_at, 1.0, 0.0), axis=1, keepdims=True)
    listed[...] = jnp.broadcast_to(hits, (CAP, BLK))

    for axis in range(4):
        head[axis] = state[axis, SHARE : 2 * SHARE, :]

    density[...] = scaled

    def tail_row(row, carry):
        at = jnp.clip(filled - SHARE, 0, CAP - SHARE) + row
        for axis in range(3):
            tail[axis, pl.ds(row, 1), :] = pos_ref[axis, pl.ds(at, 1), :]
        tail[3, pl.ds(row, 1), :] = density[pl.ds(at, 1), :]
        return carry

    lax.fori_loop(0, SHARE, tail_row, 0, unroll=4)

    hood_z[FIELD_NULL : FIELD_NULL + 8, :] = jnp.zeros((8, BLK), jnp.float32)
    hood_t[FIELD_NULL : FIELD_NULL + 8, :] = jnp.zeros((8, BLK), jnp.float32)

    def place_row(row, carry):
        order = first + row - SHARE
        slot = order - start
        inside = (order >= 0) & (order < total)
        at = jnp.where(slot < filled, SHARE + slot, SHARE + CAP + slot - filled)
        state_at[row] = jnp.where(inside, jnp.clip(at, 0, STATE_NULL - 1), STATE_NULL)
        at = jnp.where(slot < 0, before + slot - SHARE, 3 * SHARE + slot)
        at = jnp.where(slot < filled, at, 3 * SHARE + CAP + slot - filled)
        field_at[row] = jnp.where(inside, jnp.clip(at, 0, FIELD_NULL - 1), FIELD_NULL)
        return carry

    lax.fori_loop(0, HOOD, place_row, 0, unroll=2)

    @pl.when(column == 0)
    def _():
        pl.semaphore_wait(barrier, 2 + 3 + 7 + 15 + 3)

    @pl.when(column > 0)
    def _():
        pl.semaphore_wait(barrier, 2 + 3 + 7 + 15 + 1)

    def remote(source, target, send, recv, device):
        return pltpu.make_async_remote_copy(
            src_ref=source, dst_ref=target, send_sem=send, recv_sem=recv, device_id=device, device_id_type=MESH
        )

    to_after = remote(tail, state.at[:, 0:SHARE, :], state_send.at[0], state_recv.at[0], (after, column))
    to_ahead = remote(head, state.at[:, SHARE + CAP : 2 * SHARE + CAP, :], state_send.at[1], state_recv.at[1], (ahead, column))
    to_after.start()
    to_ahead.start()
    list_copies = []
    for step in range(1, columns):
        other = lax.rem(column + step, columns)
        copy = remote(
            listed.at[pl.ds(pl.multiple_of(other * SHARE, SHARE), SHARE), :],
            listed_in.at[step - 1],
            list_send.at[step - 1],
            list_recv.at[step - 1],
            (piece, other),
        )
        copy.start()
        list_copies.append(copy)
    to_after.wait()
    to_ahead.wait()
    for copy in list_copies:
        copy.wait()
    mine = listed[pl.ds(pl.multiple_of(column * SHARE, SHARE), SHARE), :]
    for step in range(columns - 1):
        mine = mine + listed_in[step]
    listed_in[0] = mine

    lane = lax.broadcasted_iota(jnp.int32, (8, BLK), 1)
    sublane = lax.broadcasted_iota(jnp.int32, (8, BLK), 0)

    def to_row(block):
        return jnp.sum(block.T, axis=0, keepdims=True)

    origin_at = state_at[SHARE]
    origins = [state[axis, pl.ds(origin_at, 1), :][:, 0:1] for axis in range(3)]
    for axis in range(3):
        state[axis, STATE_NULL : STATE_NULL + 8, :] = jnp.broadcast_to(origins[axis] + FAR, (8, BLK))
    state[3, STATE_NULL : STATE_NULL + 8, :] = jnp.full((8, BLK), 64.0, jnp.float32)

    def hood_row(row, carry):
        for axis in range(4):
            hood_state[axis, pl.ds(row, 1), :] = state[axis, pl.ds(state_at[row], 1), :]
        return carry

    lax.fori_loop(0, HOOD, hood_row, 0, unroll=8)

    def parts(value, count):
        out = []
        for _ in range(count):
            out.append(value.astype(jnp.bfloat16).astype(jnp.float32))
            value = value - out[-1]
        return out

    def rows_at(row0, size):
        rows = slice(row0, row0 + size)
        coarse, middle, fine = [], [], []
        for axis in range(3):
            shifted = hood_state[axis, rows, :] - origins[axis]
            big = jnp.floor(shifted * 16.0 + 0.5) * 0.0625
            mid, low = parts(shifted - big, 2)
            coarse.append(big)
            middle.append(mid)
            fine.append(low)
        square = sum(big * big for big in coarse)
        rest = sum(
            (2.0 * big + (mid + low)) * (mid + low) for big, mid, low in zip(coarse, middle, fine)
        )
        return coarse, middle, fine, parts(square, 2), rest, parts(hood_state[3, rows, :], 3)

    def put(target, size, row0, feature, value):
        target[feature * size + row0 : feature * size + row0 + 8, :] = value

    one = jnp.ones((8, BLK), jnp.float32)
    zero = jnp.zeros((8, BLK), jnp.float32)
    for row0 in range(0, HOOD, 8):
        coarse, middle, fine, square, rest, rho = rows_at(row0, 8)
        values = coarse + [one, one] + square + [zero]
        values += middle + coarse + middle + fine + coarse + fine + middle
        values += [one] * 3 + parts(rest, 3)
        values += [zero] * (FEATURES - len(values))
        for feature, value in enumerate(values):
            put(right_rows, HOOD, row0, feature, value)
        values = [zero] * 3 + [one] * 3 + rho + [zero] * 7
        for feature, value in enumerate(values):
            put(rho_rows, HOOD, row0, feature, value)
        if SHARE <= row0 < 2 * SHARE:
            c2, m2, f2 = ([-2.0 * value for value in group] for group in (coarse, middle, fine))
            values = c2 + square + [one, one] + [zero]
            values += c2 + m2 + m2 + c2 + f2 + m2 + f2
            values += parts(rest + 0.01, 3) + [one] * 3
            values += rho + [one] * 3
            values += [zero] * (FEATURES - len(values))
            for feature, value in enumerate(values):
                put(left_rows, SHARE, row0 - SHARE, feature, value)

    def pack_right(row, carry):
        right[row, :, 0:BLK] = right_rows[pl.ds(row, FEATURES, stride=HOOD), :].astype(jnp.bfloat16)
        right[row, 0:32, BLK : 2 * BLK] = jnp.zeros((32, BLK), jnp.bfloat16)
        right[row, 32:48, BLK : 2 * BLK] = rho_rows[pl.ds(row, 16, stride=HOOD), :].astype(jnp.bfloat16)
        return carry

    lax.fori_loop(0, HOOD, pack_right, 0, unroll=4)

    def pack_left(row, carry):
        left[row] = left_rows[pl.ds(row, FEATURES, stride=SHARE), :].T.astype(jnp.bfloat16)
        return carry

    lax.fori_loop(0, SHARE, pack_left, 0, unroll=4)

    def unit_at(unit):
        rank = unit // 2
        cell = pattern[rank * CELL_STEP]
        own = ((cell - first) & (LAYER - 1)) + LAYER * lax.rem(unit, 2)
        base = ((first + own) & ~(LAYER - 1)) - first + SHARE
        return rank * CELL_STEP, own, base

    def sources(place, base, degree):
        return [
            base + step * LAYER + pattern[place + k] for step in (0, -1, 1) for k in range(degree)
        ]

    for degree, unit_first, units, tile_first in GROUPS:

        def weigh_body(index, carry, degree=degree, unit_first=unit_first, tile_first=tile_first):
            unit = unit_first + index
            place, own, base = unit_at(unit)
            mine = left[own]
            tile = tile_first + index * (3 * degree)
            often = jnp.broadcast_to(listed_in[0, pl.ds(own, 1), :], (8, BLK))
            sums = [None] * 16
            for k, at in enumerate(sources(place, base, degree)):
                both = jnp.dot(mine, right[at], preferred_element_type=jnp.float32)
                for group in range(16):
                    rows = slice(8 * group, 8 * group + 8)
                    apart = both[rows, 0:BLK]
                    near_by = jnp.maximum(1.01 - apart, 0.0)
                    weight = near_by * near_by * (1.0 / (apart * both[rows, BLK : 2 * BLK]))
                    if k == 0:
                        weight = jnp.where(sublane + 8 * group == lane, 0.0, weight * often)
                        sums[group] = weight
                    else:
                        sums[group] = sums[group] + weight
                    tiles[tile + k, rows, :] = weight
            rowbuf[pl.ds(unit, 1), :] = to_row(jnp.concatenate(sums, axis=0))
            return carry

        lax.fori_loop(0, units, weigh_body, 0)

    spots = []
    for spot in range(SHARE):
        rank = rank_of[(first + spot) & (LAYER - 1)]
        spots.append(2 * rank + spot // LAYER)

    def settle():
        return jnp.concatenate([rowbuf[pl.ds(spot, 1), :] for spot in spots], axis=0)

    own_at = pl.multiple_of(SHARE * column, SHARE)
    alive = lax.broadcasted_iota(jnp.int32, (SHARE, BLK), 0) + own_at < filled
    diagonal = 64.0 / hood_state[3, SHARE : 2 * SHARE, :] + settle()
    diag[...] = diagonal
    source = jnp.where(alive, rhs_ref[...], 0.0)
    z = jnp.where(alive, source / diagonal, 0.0)

    def exchange(own, hood, send, recv):
        source_ref = own

        def chunk(at):
            return hood.at[pl.ds(pl.multiple_of(at, SHARE), SHARE), :]

        here = 3 * SHARE + SHARE * column
        cases = []
        cases.append((column < columns - 1, here, (piece, column + 1), 0, 0))
        cases.append((column > 0, here, (piece, column - 1), 1, 1))
        for other in range(1, columns):
            cases.append((column == 0, 3 * SHARE + CAP, (ahead, other), 1 + other, 2))
        for other in range(1, columns):
            cases.append((column == other, SHARE * (other - 1), (after, 0), 2, 2 + other))
        return source_ref, chunk, here, cases

    def start_exchange(own, hood, send, recv):
        source_ref, chunk, here, cases = exchange(own, hood, send, recv)
        for when, at, device, send_at, recv_at in cases:
            @pl.when(when)
            def _(at=at, device=device, send_at=send_at, recv_at=recv_at):
                remote(source_ref, chunk(at), send.at[send_at], recv.at[recv_at], device).start()

    def finish_exchange(own, hood, send, recv):
        source_ref, chunk, here, cases = exchange(own, hood, send, recv)
        arrive = [
            (column > 0, here - SHARE, 0),
            (column < columns - 1, here + SHARE, 1),
            (column > 0, 3 * SHARE + CAP, 2),
        ]
        for other in range(1, columns):
            arrive.append((column == 0, SHARE * (other - 1), 2 + other))
        for when, at, recv_at in arrive:
            @pl.when(when)
            def _(at=at, recv_at=recv_at):
                remote(source_ref, chunk(at), send.at[0], recv.at[recv_at], (after, column)).wait_recv()

        for when, at, device, send_at, recv_at in cases:
            @pl.when(when)
            def _(at=at, device=device, send_at=send_at, recv_at=recv_at):
                remote(source_ref, chunk(at), send.at[send_at], recv.at[recv_at], device).wait_send()

    def product(value, own, hood, send, recv):
        own[...] = value
        start_exchange(own, hood, send, recv)
        hood[pl.ds(pl.multiple_of(3 * SHARE + own_at, SHARE), SHARE), :] = value

        finish_exchange(own, hood, send, recv)

        def field_row(row, carry):
            near_field[pl.ds(row, 1), :] = hood[pl.ds(field_at[row], 1), :]
            return carry

        lax.fori_loop(0, HOOD, field_row, 0, unroll=8)

        for degree, unit_first, units, tile_first in GROUPS:

            def unit_body(index, carry, degree=degree, unit_first=unit_first, tile_first=tile_first):
                unit = unit_first + index
                place, own_spot, base = unit_at(unit)
                tile = tile_first + index * (3 * degree)
                fields = [
                    jnp.broadcast_to(near_field[pl.ds(at, 1), :], (8, BLK)) for at in sources(place, base, degree)
                ]
                sums = []
                for group in range(16):
                    rows = slice(8 * group, 8 * group + 8)
                    total = tiles[tile, rows, :] * fields[0]
                    for k in range(1, 3 * degree):
                        total = total + tiles[tile + k, rows, :] * fields[k]
                    sums.append(total)
                rowbuf[pl.ds(unit, 1), :] = to_row(jnp.concatenate(sums, axis=0))
                return carry

            lax.fori_loop(0, units, unit_body, 0, unroll=2)

    product(z, own_z, hood_z, z_send, z_recv)
    y0[...] = jnp.where(alive, settle(), 0.0)
    t = jnp.where(alive, y0[...] / diag[...], 0.0)
    product(t, own_t, hood_t, t_send, t_recv)
    y1[...] = jnp.where(alive, settle(), 0.0)

    z = own_z[...]
    t = own_t[...]
    source = jnp.where(alive, rhs_ref[...], 0.0)

    def partial(first, second):
        return jnp.sum(first * second, axis=0, keepdims=True)

    moments[0:1, :] = partial(source, z)
    moments[1:2, :] = partial(z, y0[...])
    moments[2:3, :] = partial(y0[...], t)
    moments[3:4, :] = partial(t, y1[...])
    moments[4:8, :] = jnp.zeros((4, BLK), jnp.float32)

    def share_sums(from_ref, stage, rank, size, member, send, recv):
        copies = []
        for step in range(1, size):
            copy = remote(
                from_ref, stage.at[rank], send.at[step - 1], recv.at[step - 1], member(lax.rem(rank + step, size))
            )
            copy.start()
            copies.append(copy)
        stage[rank] = from_ref[...]
        for copy in copies:
            copy.wait()
        total = stage[0]
        for k in range(1, size):
            total = total + stage[k]
        return total

    moments[8:16, :] = share_sums(moments.at[0:8, :], stage_a, rank_a, 8, member_a, a_send, a_recv)
    total = share_sums(moments.at[8:16, :], stage_b, chip, 16, member_b, b_send, b_recv)
    sums = jnp.sum(total, axis=1, keepdims=True)
    e0, e1, e2, e3 = (sums[k : k + 1, :] for k in range(4))
    f1 = e1 / e0
    f2 = e2 / e0
    f3 = e3 / e0
    lead = 1.0 / (1.0 - f1)
    spread_of = f2 - f1 * f1
    ratio = lead * lead * spread_of
    bent = f3 - 2.0 * f1 * f2 + f1 * f1 * f1
    second = spread_of / (spread_of - bent - lead * spread_of * spread_of)
    mix = ratio - lead * f1
    first_image = y0[...]
    direction = lead * t + mix * z
    x_ref[...] = lead * z + second * direction
    image = (lead - mix) * first_image + mix * source - lead * y1[...]
    r_ref[...] = lead * (first_image - f1 * source) - second * image


def body(positions, phase, neighbours, counts, phase_density, right_side):
    pieces = lax.axis_size("piece")
    columns = lax.axis_size("col")
    vmem = pl.BlockSpec(memory_space=pltpu.VMEM)
    smem = pl.BlockSpec(memory_space=pltpu.SMEM)
    f32 = jnp.float32
    dma = pltpu.SemaphoreType.DMA
    shape = jax.ShapeDtypeStruct((SHARE, BLK), f32)
    return pl.pallas_call(
        functools.partial(kernel, pieces, columns),
        out_shape=(shape, shape),
        in_specs=[smem, smem, vmem, vmem, vmem, vmem],
        out_specs=(vmem, vmem),
        scratch_shapes=[
            pltpu.SMEM((LAYER * CELL_STEP,), jnp.int32),
            pltpu.SMEM((LAYER,), jnp.int32),
            pltpu.SMEM((HOOD,), jnp.int32),
            pltpu.SMEM((HOOD,), jnp.int32),
            pltpu.VMEM((4, STATE_NULL + 8, BLK), f32),
            pltpu.VMEM((4, HOOD, BLK), f32),
            pltpu.VMEM((FEATURES * HOOD, BLK), f32),
            pltpu.VMEM((16 * HOOD, BLK), f32),
            pltpu.VMEM((FEATURES * SHARE, BLK), f32),
            pltpu.VMEM((HOOD, FEATURES, 2 * BLK), jnp.bfloat16),
            pltpu.VMEM((SHARE, BLK, FEATURES), jnp.bfloat16),
            pltpu.VMEM((TILES, BLK, BLK), f32),
            pltpu.VMEM((CAP, BLK), f32),
            pltpu.VMEM((3, SHARE, BLK), f32),
            pltpu.VMEM((4, SHARE, BLK), f32),
            pltpu.VMEM((4, SHARE, BLK), f32),
            pltpu.VMEM((CAP, BLK), f32),
            pltpu.VMEM((SHARE, BLK), f32),
            pltpu.VMEM((SHARE, BLK), f32),
            pltpu.VMEM((FIELD_NULL + 8, BLK), f32),
            pltpu.VMEM((FIELD_NULL + 8, BLK), f32),
            pltpu.VMEM((HOOD, BLK), f32),
            pltpu.VMEM((UNITS, BLK), f32),
            pltpu.VMEM((SHARE, BLK), f32),
            pltpu.VMEM((SHARE, BLK), f32),
            pltpu.VMEM((SHARE, BLK), f32),
            pltpu.VMEM((16, BLK), f32),
            pltpu.VMEM((8, 8, BLK), f32),
            pltpu.VMEM((16, 8, BLK), f32),
            dma((2,)), dma((2,)), dma((3,)), dma((3,)),
            dma((5,)), dma((6,)), dma((5,)), dma((6,)),
            dma((7,)), dma((7,)), dma((15,)), dma((15,)),
        ],
        compiler_params=pltpu.CompilerParams(
            collective_id=0, has_side_effects=True, vmem_limit_bytes=60 * 1024 * 1024
        ),
        name="pressure",
    )(counts, phase_density, positions, phase, neighbours, right_side)


def solution(mesh):
    placed = (
        P(None, "piece", None),
        P("piece", None),
        P("piece", "col"),
        P(),
        P(),
        P(("piece", "col"), None),
    )
    return jax.shard_map(
        body,
        mesh=mesh,
        in_specs=placed,
        out_specs=(P(("piece", "col"), None), P(("piece", "col"), None)),
        check_vma=False,
    )
```

```python
import functools

import jax
import jax.numpy as jnp
from jax import lax
from jax.experimental import pallas as pl
from jax.experimental.pallas import tpu as pltpu
from jax.sharding import PartitionSpec as P

MESH = pl.DeviceIdType.MESH
BLK = 128
CAP = 128
LAYER = 16
SHARE = 32
HOOD = 3 * SHARE
FEATURES = 48
FAR = 64.0
STATE_NULL = 192
FIELD_NULL = 256
CELL_STEP = 10


def layer_cells():
    place = []
    for code in range(LAYER):
        across = code % 2 + 2 * (code // 4 % 2)
        along = code // 2 % 2 + 2 * (code // 8 % 2)
        place.append((across, along))
    near = []
    for code in range(LAYER):
        others = [
            other
            for other in range(LAYER)
            if other != code
            and abs(place[other][0] - place[code][0]) <= 1
            and abs(place[other][1] - place[code][1]) <= 1
        ]
        near.append([code] + others)
    return near


NEAR = layer_cells()
CELLS = sorted(range(LAYER), key=lambda code: (len(NEAR[code]), code))


def unit_plan():
    groups, first_unit, first_tile = [], 0, 0
    for degree in (4, 6, 9):
        units = 2 * len([code for code in CELLS if len(NEAR[code]) == degree])
        groups.append((degree, first_unit, units, first_tile))
        first_unit += units
        first_tile += 3 * degree * units
    return groups, first_unit, first_tile


GROUPS, UNITS, TILES = unit_plan()
PATTERN = [0] * (LAYER * CELL_STEP)
RANK_OF = [0] * LAYER
for _rank, _code in enumerate(CELLS):
    RANK_OF[_code] = _rank
    PATTERN[_rank * CELL_STEP : _rank * CELL_STEP + len(NEAR[_code])] = NEAR[_code]


def kernel(
    pieces, columns,
    counts, dens, pos_ref, phase_ref, near_ref, rhs_ref,
    x_ref, r_ref,
    pattern, rank_of, state_at, field_at,
    state, hood_state, right_rows, rho_rows, left_rows, right, left, tiles, accs,
    hits, hits_in, often, rhs_all, head, tail, density,
    own_z, own_t, hood_z, hood_t, near_field, rowbuf, diag, y0, y1, source_at, final, first_field, moments, stage_a, stage_b,
    state_send, state_recv, hits_send, hits_recv, rhs_send, rhs_recv, z_send, z_recv, t_send, t_recv, a_send, a_recv, b_send, b_recv,
):
    piece = lax.axis_index("piece")
    column = lax.axis_index("col")
    after = lax.rem(piece + 1, pieces)
    ahead = lax.rem(piece + pieces - 1, pieces)
    core = lax.rem(piece, 2)
    chip = piece // 2
    rank_a = column * 2 + core

    def member_a(rank):
        return (chip * 2 + lax.rem(rank, 2), rank // 2)

    def member_b(rank):
        return (rank * 2 + core, column)

    barrier = pltpu.get_barrier_semaphore()

    def greet(target):
        pl.semaphore_signal(barrier, inc=1, device_id=target, device_id_type=MESH)

    greet((after, column))
    greet((ahead, column))
    for step in range(1, columns):
        greet((piece, lax.rem(column + step, columns)))
    for step in range(1, 8):
        greet(member_a(lax.rem(rank_a + step, 8)))
    for step in range(1, 16):
        greet(member_b(lax.rem(chip + step, 16)))

    @pl.when(column == 0)
    def _():
        for other in range(1, columns):
            greet((ahead, other))

    @pl.when(column > 0)
    def _():
        greet((after, 0))

    start, total, filled, before = 0, 0, 0, 0
    for other in range(pieces):
        count = counts[other]
        start = start + jnp.where(other < piece, count, 0)
        total = total + count
        filled = filled + jnp.where(other == piece, count, 0)
        before = before + jnp.where(other == piece - 1, count, 0)
    own_first = SHARE * column
    frame = jnp.clip(jnp.minimum(own_first, filled - SHARE), 0, CAP - SHARE)
    first = start + frame
    for place, code in enumerate(PATTERN):
        pattern[place] = code
    for code in range(LAYER):
        rank_of[code] = RANK_OF[code]

    phase = phase_ref[...]
    scaled = jnp.where(phase == 0, dens[0], jnp.where(phase == 1, dens[1], dens[2])) * 64.0
    density[...] = scaled
    for axis in range(3):
        state[axis, SHARE : SHARE + CAP, :] = pos_ref[axis]
    state[3, SHARE : SHARE + CAP, :] = scaled

    near = near_ref[...]
    me_at = lax.broadcasted_iota(jnp.int32, near.shape, 1) + piece * CAP
    hits[0:1, :] = jnp.sum(jnp.where(near == me_at, 1.0, 0.0), axis=0, keepdims=True)

    for axis in range(4):
        head[axis] = pos_ref[axis, 0:SHARE, :] if axis < 3 else scaled[0:SHARE, :]

    density[...] = scaled

    def tail_row(row, carry):
        at = jnp.clip(filled - SHARE, 0, CAP - SHARE) + row
        for axis in range(3):
            tail[axis, pl.ds(row, 1), :] = pos_ref[axis, pl.ds(at, 1), :]
        tail[3, pl.ds(row, 1), :] = density[pl.ds(at, 1), :]
        return carry

    lax.fori_loop(0, SHARE, tail_row, 0, unroll=4)

    hood_z[FIELD_NULL : FIELD_NULL + 8, :] = jnp.zeros((8, BLK), jnp.float32)
    hood_t[FIELD_NULL : FIELD_NULL + 8, :] = jnp.zeros((8, BLK), jnp.float32)

    def place_row(row, carry):
        order = first + row - SHARE
        slot = order - start
        inside = (order >= 0) & (order < total)
        at = jnp.where(slot < filled, SHARE + slot, SHARE + CAP + slot - filled)
        state_at[row] = jnp.where(inside, jnp.clip(at, 0, STATE_NULL - 1), STATE_NULL)
        at = jnp.where(slot < 0, before + slot - SHARE, 3 * SHARE + slot)
        at = jnp.where(slot < filled, at, 3 * SHARE + CAP + slot - filled)
        field_at[row] = jnp.where(inside, jnp.clip(at, 0, FIELD_NULL - 1), FIELD_NULL)
        return carry

    lax.fori_loop(0, HOOD, place_row, 0, unroll=2)

    lane = lax.broadcasted_iota(jnp.int32, (8, BLK), 1)
    sublane = lax.broadcasted_iota(jnp.int32, (8, BLK), 0)

    def to_row(block):
        return jnp.sum(block.T, axis=0, keepdims=True)

    def frame_row(row, carry):
        for axis in range(3):
            hood_state[axis, pl.ds(SHARE + row, 1), :] = pos_ref[axis, pl.ds(frame + row, 1), :]
        hood_state[3, pl.ds(SHARE + row, 1), :] = density[pl.ds(frame + row, 1), :]
        return carry

    lax.fori_loop(0, SHARE, frame_row, 0, unroll=8)
    origins = [hood_state[axis, SHARE : SHARE + 1, 0:1] for axis in range(3)]

    def parts(value, count):
        out = []
        for _ in range(count):
            out.append(value.astype(jnp.bfloat16).astype(jnp.float32))
            value = value - out[-1]
        return out

    def rows_at(row0, size):
        rows = slice(row0, row0 + size)
        coarse, middle, fine = [], [], []
        for axis in range(3):
            shifted = hood_state[axis, rows, :] - origins[axis]
            big = jnp.floor(shifted * 16.0 + 0.5) * 0.0625
            mid, low = parts(shifted - big, 2)
            coarse.append(big)
            middle.append(mid)
            fine.append(low)
        square = sum(big * big for big in coarse)
        rest = sum(
            (2.0 * big + (mid + low)) * (mid + low) for big, mid, low in zip(coarse, middle, fine)
        )
        return coarse, middle, fine, parts(square, 2), rest, parts(hood_state[3, rows, :], 3)

    one = jnp.ones((8, BLK), jnp.float32)
    zero = jnp.zeros((8, BLK), jnp.float32)

    def put(target, count, row0, values):
        for feature in range(count):
            at = (row0 // 8 * count + feature) * 8
            target[at : at + 8, :] = values[feature] if feature < len(values) else zero

    def build_rows(starts):
        for row0 in starts:
            coarse, middle, fine, square, rest, rho = rows_at(row0, 8)
            values = coarse + [one, one] + square + [zero]
            values += middle + coarse + middle + fine + coarse + fine + middle
            values += [one] * 3 + parts(rest, 3)
            put(right_rows, FEATURES, row0, values)
            put(rho_rows, 16, row0, [zero] * 3 + [one] * 3 + rho)
            if SHARE <= row0 < 2 * SHARE:
                c2, m2, f2 = ([-2.0 * value for value in group] for group in (coarse, middle, fine))
                values = c2 + square + [one, one] + [zero]
                values += c2 + m2 + m2 + c2 + f2 + m2 + f2
                values += parts(rest + 0.01, 3) + [one] * 3
                values += rho + [one] * 3
                put(left_rows, FEATURES, row0 - SHARE, values)

    def pack_right(row, carry):
        group, inner = row // 8, lax.rem(row, 8)
        right[row, :, 0:BLK] = right_rows[pl.ds(group * (8 * FEATURES) + inner, FEATURES, stride=8), :].astype(jnp.bfloat16)
        right[row, 0:32, BLK : 2 * BLK] = jnp.zeros((32, BLK), jnp.bfloat16)
        right[row, 32:48, BLK : 2 * BLK] = rho_rows[pl.ds(group * 128 + inner, 16, stride=8), :].astype(jnp.bfloat16)
        return carry

    def pack_left(row, carry):
        group, inner = row // 8, lax.rem(row, 8)
        left[row] = left_rows[pl.ds(group * (8 * FEATURES) + inner, FEATURES, stride=8), :].T.astype(jnp.bfloat16)
        return carry

    build_rows(range(SHARE, 2 * SHARE, 8))
    lax.fori_loop(SHARE, 2 * SHARE, pack_right, 0, unroll=4)
    lax.fori_loop(0, SHARE, pack_left, 0, unroll=4)

    def unit_at(unit):
        rank = unit // 2
        place = rank * CELL_STEP
        half = LAYER * lax.rem(unit, 2)
        own = ((pattern[place] - first) & (LAYER - 1)) + half
        base = ((first + own) & ~(LAYER - 1)) - first + SHARE
        return place, half, own, base

    def mates(place, half, degree):
        return [((pattern[place + k] - first) & (LAYER - 1)) + half + SHARE for k in range(degree)]

    def others(place, half, base, degree):
        lower, upper = [], []
        for k, mate in enumerate(mates(place, half, degree)):
            level = base + pattern[place + k]
            lower.append(level - jnp.where(mate < level, 0, LAYER))
            upper.append(level + jnp.where(mate > level, 0, LAYER))
        return lower + upper

    def weigh(mine, at, tile, sums, multiply):
        both = jnp.dot(mine, right[at], preferred_element_type=jnp.float32)
        out = []
        for group in range(16):
            rows = slice(8 * group, 8 * group + 8)
            apart = both[rows, 0:BLK]
            near_by = jnp.maximum(1.01 - apart, 0.0)
            weight = near_by * near_by * (1.0 / (apart * both[rows, BLK : 2 * BLK]))
            if multiply is not None:
                weight = jnp.where(sublane + 8 * group == lane, 0.0, weight * multiply)
            tiles[tile, rows, :] = weight
            out.append(weight if sums is None else sums[group] + weight)
        return out

    @pl.when(column == 0)
    def _():
        pl.semaphore_wait(barrier, 2 + 3 + 7 + 15 + 3)

    @pl.when(column > 0)
    def _():
        pl.semaphore_wait(barrier, 2 + 3 + 7 + 15 + 1)

    def remote(source, target, send, recv, device):
        return pltpu.make_async_remote_copy(
            src_ref=source, dst_ref=target, send_sem=send, recv_sem=recv, device_id=device, device_id_type=MESH
        )

    to_after = remote(tail, state.at[:, 0:SHARE, :], state_send.at[0], state_recv.at[0], (after, column))
    to_ahead = remote(head, state.at[:, SHARE + CAP : 2 * SHARE + CAP, :], state_send.at[1], state_recv.at[1], (ahead, column))
    to_after.start()
    to_ahead.start()
    early = [to_after, to_ahead]
    own_at = pl.multiple_of(own_first, SHARE)
    for step in range(1, columns):
        other = lax.rem(column + step, columns)
        early.append(
            remote(hits.at[0:1, :], hits_in.at[step - 1, 0:1, :], hits_send.at[step - 1], hits_recv.at[step - 1], (piece, other))
        )
        early.append(
            remote(rhs_ref, rhs_all.at[pl.ds(own_at, SHARE), :], rhs_send.at[step - 1], rhs_recv.at[step - 1], (piece, other))
        )
    for copy in early[2:]:
        copy.start()
    rhs_all[pl.ds(own_at, SHARE), :] = rhs_ref[...]

    for degree, unit_first, units, tile_first in GROUPS:

        def near_body(index, carry, degree=degree, unit_first=unit_first, tile_first=tile_first):
            unit = unit_first + index
            place, half, own, base = unit_at(unit)
            mine = left[own]
            tile = tile_first + index * (3 * degree)
            sums = None
            for k, at in enumerate(mates(place, half, degree)):
                if k > 0:
                    sums = weigh(mine, at, tile + k, sums, None)
            for group in range(16):
                accs[unit, 8 * group : 8 * group + 8, :] = sums[group]
            return carry

        lax.fori_loop(0, units, near_body, 0, unroll=2 if degree < 9 else 1)

    for copy in early:
        copy.wait()
    total_hits = hits[0:1, :]
    for step in range(columns - 1):
        total_hits = total_hits + hits_in[step, 0:1, :]
    often[...] = jnp.broadcast_to(total_hits, (CAP, BLK)).T

    for axis in range(3):
        state[axis, STATE_NULL : STATE_NULL + 8, :] = jnp.broadcast_to(origins[axis] + FAR, (8, BLK))
    state[3, STATE_NULL : STATE_NULL + 8, :] = jnp.full((8, BLK), 64.0, jnp.float32)

    def hood_row(index, carry):
        row = index + SHARE * (index // SHARE)
        for axis in range(4):
            hood_state[axis, pl.ds(row, 1), :] = state[axis, pl.ds(state_at[row], 1), :]
        return carry

    lax.fori_loop(0, 2 * SHARE, hood_row, 0, unroll=8)
    build_rows([row for row in range(0, HOOD, 8) if not SHARE <= row < 2 * SHARE])
    lax.fori_loop(0, SHARE, pack_right, 0, unroll=4)
    lax.fori_loop(2 * SHARE, HOOD, pack_right, 0, unroll=4)

    for degree, unit_first, units, tile_first in GROUPS:

        def far_body(index, carry, degree=degree, unit_first=unit_first, tile_first=tile_first):
            unit = unit_first + index
            place, half, own, base = unit_at(unit)
            mine = left[own]
            tile = tile_first + index * (3 * degree)
            listed = jnp.broadcast_to(often[pl.ds(frame + own, 1), :], (8, BLK))
            sums = [accs[unit, 8 * group : 8 * group + 8, :] for group in range(16)]
            sums = weigh(mine, SHARE + own, tile, sums, listed)
            for k, at in enumerate(others(place, half, base, degree)):
                sums = weigh(mine, at, tile + degree + k, sums, None)
            rowbuf[pl.ds(unit, 1), :] = to_row(jnp.concatenate(sums, axis=0))
            return carry

        lax.fori_loop(0, units, far_body, 0)


    spots = []
    for spot in range(SHARE):
        rank = rank_of[(first + spot) & (LAYER - 1)]
        spots.append(2 * rank + spot // LAYER)

    def settle():
        return jnp.concatenate([rowbuf[pl.ds(spot, 1), :] for spot in spots], axis=0)

    spot_at = lax.broadcasted_iota(jnp.int32, (SHARE, BLK), 0)
    mine_here = (spot_at + frame >= own_first) & (spot_at + frame < own_first + SHARE)
    diag[...] = 64.0 / hood_state[3, SHARE : 2 * SHARE, :] + settle()
    for spot in range(SHARE):
        source_at[spot : spot + 1, :] = rhs_all[pl.ds(frame + spot, 1), :]

    own_live = spot_at + own_first < filled

    def to_own(ref):
        places = [jnp.clip(own_first + spot - frame, 0, SHARE - 1) for spot in range(SHARE)]
        rows = jnp.concatenate([ref[pl.ds(place, 1), :] for place in places], axis=0)
        return jnp.where(own_live, rows, 0.0)

    def exchange(own, hood, send, recv):
        source_ref = own

        def chunk(at):
            return hood.at[pl.ds(pl.multiple_of(at, SHARE), SHARE), :]

        here = 3 * SHARE + SHARE * column
        cases = []
        cases.append((column < columns - 1, here, (piece, column + 1), 0, 0))
        cases.append((column > 0, here, (piece, column - 1), 1, 1))
        cases.append((column < columns - 2, here, (piece, column + 2), 5, 6))
        for other in range(1, columns):
            cases.append((column == 0, 3 * SHARE + CAP, (ahead, other), 1 + other, 2))
        for other in range(1, columns):
            cases.append((column == other, SHARE * (other - 1), (after, 0), 2, 2 + other))
        return source_ref, chunk, here, cases

    def start_exchange(own, hood, send, recv):
        source_ref, chunk, here, cases = exchange(own, hood, send, recv)
        for when, at, device, send_at, recv_at in cases:
            @pl.when(when)
            def _(at=at, device=device, send_at=send_at, recv_at=recv_at):
                remote(source_ref, chunk(at), send.at[send_at], recv.at[recv_at], device).start()

    def finish_exchange(own, hood, send, recv):
        source_ref, chunk, here, cases = exchange(own, hood, send, recv)
        arrive = [
            (column > 0, here - SHARE, 0),
            (column < columns - 1, here + SHARE, 1),
            (column > 0, 3 * SHARE + CAP, 2),
            (column > 1, here - 2 * SHARE, 6),
        ]
        for other in range(1, columns):
            arrive.append((column == 0, SHARE * (other - 1), 2 + other))
        for when, at, recv_at in arrive:
            @pl.when(when)
            def _(at=at, recv_at=recv_at):
                remote(source_ref, chunk(at), send.at[0], recv.at[recv_at], (after, column)).wait_recv()

        for when, at, device, send_at, recv_at in cases:
            @pl.when(when)
            def _(at=at, device=device, send_at=send_at, recv_at=recv_at):
                remote(source_ref, chunk(at), send.at[send_at], recv.at[recv_at], device).wait_send()

    def product(value, own, hood, send, recv):
        near_field[SHARE : 2 * SHARE, :] = value
        final[...] = value
        own[...] = to_own(final)
        start_exchange(own, hood, send, recv)

        def fields_at(sources):
            return [jnp.broadcast_to(near_field[pl.ds(at, 1), :], (8, BLK)) for at in sources]

        for degree, unit_first, units, tile_first in GROUPS:

            def first_body(index, carry, degree=degree, unit_first=unit_first, tile_first=tile_first):
                unit = unit_first + index
                place, half, own_spot, base = unit_at(unit)
                tile = tile_first + index * (3 * degree)
                fields = fields_at(mates(place, half, degree))
                for group in range(16):
                    rows = slice(8 * group, 8 * group + 8)
                    total = tiles[tile, rows, :] * fields[0]
                    for k in range(1, degree):
                        total = total + tiles[tile + k, rows, :] * fields[k]
                    accs[unit, rows, :] = total
                return carry

            lax.fori_loop(0, units, first_body, 0, unroll=2)

        finish_exchange(own, hood, send, recv)

        def field_row(index, carry):
            row = index + SHARE * (index // SHARE)
            near_field[pl.ds(row, 1), :] = hood[pl.ds(field_at[row], 1), :]
            return carry

        lax.fori_loop(0, 2 * SHARE, field_row, 0, unroll=8)

        for degree, unit_first, units, tile_first in GROUPS:

            def unit_body(index, carry, degree=degree, unit_first=unit_first, tile_first=tile_first):
                unit = unit_first + index
                place, half, own_spot, base = unit_at(unit)
                tile = tile_first + index * (3 * degree) + degree
                fields = fields_at(others(place, half, base, degree))
                sums = []
                for group in range(16):
                    rows = slice(8 * group, 8 * group + 8)
                    total = accs[unit, rows, :]
                    for k in range(2 * degree):
                        total = total + tiles[tile + k, rows, :] * fields[k]
                    sums.append(total)
                rowbuf[pl.ds(unit, 1), :] = to_row(jnp.concatenate(sums, axis=0))
                return carry

            lax.fori_loop(0, units, unit_body, 0, unroll=2)

    z = source_at[...] / diag[...]
    product(z, own_z, hood_z, z_send, z_recv)
    y0[...] = settle()
    t = y0[...] / diag[...]
    z = near_field[SHARE : 2 * SHARE, :]
    source = source_at[...]

    def partial(first, second):
        value = jnp.where(mine_here, first * second, 0.0)
        return jnp.sum(jnp.sum(value, axis=0, keepdims=True), axis=1, keepdims=True)

    column_at = lax.broadcasted_iota(jnp.int32, (1, BLK), 1)
    parts_row = jnp.where(column_at == 0, partial(source, z), 0.0)
    parts_row = jnp.where(column_at == 1, partial(z, y0[...]), parts_row)
    parts_row = jnp.where(column_at == 2, partial(y0[...], t), parts_row)
    first_field[...] = z
    product(t, own_t, hood_t, t_send, t_recv)
    y1[...] = settle()
    z = first_field[...]
    t = near_field[SHARE : 2 * SHARE, :]
    moments[0:1, :] = jnp.where(column_at == 3, partial(t, y1[...]), parts_row)

    def share_sums(from_ref, stage, rank, size, member, send, recv):
        copies = []
        for step in range(1, size):
            copy = remote(
                from_ref, stage.at[rank, 0:1, :], send.at[step - 1], recv.at[step - 1], member(lax.rem(rank + step, size))
            )
            copy.start()
            copies.append(copy)
        stage[rank, 0:1, :] = from_ref[...]
        for copy in copies:
            copy.wait()
        total = stage[0, 0:1, :]
        for k in range(1, size):
            total = total + stage[k, 0:1, :]
        return total

    moments[8:9, :] = share_sums(moments.at[0:1, :], stage_a, rank_a, 8, member_a, a_send, a_recv)
    total = share_sums(moments.at[8:9, :], stage_b, chip, 16, member_b, b_send, b_recv)
    e0, e1, e2, e3 = (total[0:1, k : k + 1] for k in range(4))
    f1 = e1 / e0
    f2 = e2 / e0
    f3 = e3 / e0
    lead = 1.0 / (1.0 - f1)
    spread_of = f2 - f1 * f1
    ratio = lead * lead * spread_of
    bent = f3 - 2.0 * f1 * f2 + f1 * f1 * f1
    second = spread_of / (spread_of - bent - lead * spread_of * spread_of)
    mix = ratio - lead * f1
    first_image = y0[...]
    direction = lead * t + mix * z
    source = source_at[...]
    image = (lead - mix) * first_image + mix * source - lead * y1[...]
    final[...] = lead * z + second * direction
    y1[...] = lead * (first_image - f1 * source) - second * image
    x_ref[...] = to_own(final)
    r_ref[...] = to_own(y1)


def body(positions, phase, neighbours, counts, phase_density, right_side):
    pieces = lax.axis_size("piece")
    columns = lax.axis_size("col")
    vmem = pl.BlockSpec(memory_space=pltpu.VMEM)
    smem = pl.BlockSpec(memory_space=pltpu.SMEM)
    f32 = jnp.float32
    dma = pltpu.SemaphoreType.DMA
    shape = jax.ShapeDtypeStruct((SHARE, BLK), f32)
    return pl.pallas_call(
        functools.partial(kernel, pieces, columns),
        out_shape=(shape, shape),
        in_specs=[smem, smem, vmem, vmem, vmem, vmem],
        out_specs=(vmem, vmem),
        scratch_shapes=[
            pltpu.SMEM((LAYER * CELL_STEP,), jnp.int32),
            pltpu.SMEM((LAYER,), jnp.int32),
            pltpu.SMEM((HOOD,), jnp.int32),
            pltpu.SMEM((HOOD,), jnp.int32),
            pltpu.VMEM((4, STATE_NULL + 8, BLK), f32),
            pltpu.VMEM((4, HOOD, BLK), f32),
            pltpu.VMEM((FEATURES * HOOD, BLK), f32),
            pltpu.VMEM((16 * HOOD, BLK), f32),
            pltpu.VMEM((FEATURES * SHARE, BLK), f32),
            pltpu.VMEM((HOOD, FEATURES, 2 * BLK), jnp.bfloat16),
            pltpu.VMEM((SHARE, BLK, FEATURES), jnp.bfloat16),
            pltpu.VMEM((TILES, BLK, BLK), f32),
            pltpu.VMEM((UNITS, BLK, BLK), f32),
            pltpu.VMEM((8, BLK), f32),
            pltpu.VMEM((3, 8, BLK), f32),
            pltpu.VMEM((CAP, BLK), f32),
            pltpu.VMEM((CAP, BLK), f32),
            pltpu.VMEM((4, SHARE, BLK), f32),
            pltpu.VMEM((4, SHARE, BLK), f32),
            pltpu.VMEM((CAP, BLK), f32),
            pltpu.VMEM((SHARE, BLK), f32),
            pltpu.VMEM((SHARE, BLK), f32),
            pltpu.VMEM((FIELD_NULL + 8, BLK), f32),
            pltpu.VMEM((FIELD_NULL + 8, BLK), f32),
            pltpu.VMEM((HOOD, BLK), f32),
            pltpu.VMEM((UNITS, BLK), f32),
            pltpu.VMEM((SHARE, BLK), f32),
            pltpu.VMEM((SHARE, BLK), f32),
            pltpu.VMEM((SHARE, BLK), f32),
            pltpu.VMEM((SHARE, BLK), f32),
            pltpu.VMEM((SHARE, BLK), f32),
            pltpu.VMEM((SHARE, BLK), f32),
            pltpu.VMEM((16, BLK), f32),
            pltpu.VMEM((8, 8, BLK), f32),
            pltpu.VMEM((16, 8, BLK), f32),
            dma((2,)), dma((2,)), dma((3,)), dma((3,)), dma((3,)), dma((3,)),
            dma((6,)), dma((7,)), dma((6,)), dma((7,)),
            dma((7,)), dma((7,)), dma((15,)), dma((15,)),
        ],
        compiler_params=pltpu.CompilerParams(
            collective_id=0, has_side_effects=True, vmem_limit_bytes=60 * 1024 * 1024
        ),
        name="pressure",
    )(counts, phase_density, positions, phase, neighbours.T, right_side)


def solution(mesh):
    placed = (
        P(None, "piece", None),
        P("piece", None),
        P("piece", "col"),
        P(),
        P(),
        P(("piece", "col"), None),
    )
    return jax.shard_map(
        body,
        mesh=mesh,
        in_specs=placed,
        out_specs=(P(("piece", "col"), None), P(("piece", "col"), None)),
        check_vma=False,
    )
```
